32 devices in a mesh: section: 2 (over x), ctx: 8 (over z, y), fsdp: 2 (over core).
Axes of the slice: x: 2, y: 2, z: 4, core: 2. Of those that a mesh axis runs over, the one named last changes fastest.
Arguments:
- inputs: bfloat16 [2, 2, 1024, 1024], P(None, 'fsdp', 'ctx'), may hold values from -6 to 6
- cotangent: bfloat16 [2, 2, 1024, 1024], P(None, 'fsdp', 'ctx'), may hold values from -6 to 6
- positions: int32 [2, 2, 1024], P(None, 'fsdp', 'ctx'), may hold values from 0 to 1023, as said below
- gains: bfloat16 [2, 2, 1024], P('section', None, 'fsdp'), may hold values from 0.25 to 1.75
- biases: bfloat16 [2, 6, 1024], P('section', None, 'fsdp'), may hold values from -3 to 3
- fc_bias: bfloat16 [2, 4096], P('section', 'fsdp'), may hold values from -3 to 3
- qkv_weight: bfloat16 [2, 1024, 3072], P('section', 'fsdp'), may hold values from -0.1875 to 0.1875
- out_weight: bfloat16 [2, 1024, 1024], P('section', 'fsdp'), may hold values from -3 to 3
- fc_weight: bfloat16 [2, 1024, 4096], P('section', 'fsdp'), may hold values from -0.1875 to 0.1875
- proj_weight: bfloat16 [2, 4096, 1024], P('section', 'fsdp'), may hold values from -0.09375 to 0.09375
Outputs:
- section_out: bfloat16 [2, 2, 2, 1024, 1024], P('section', None, 'fsdp', 'ctx')
- section_grad: float32 [2, 2, 2, 1024, 1024], P('section', None, 'fsdp', 'ctx')
- grad_gains: float32 [2, 2, 1024], P('section', None, 'fsdp')
- grad_biases: float32 [2, 6, 1024], P('section', None, 'fsdp')
- grad_fc_bias: float32 [2, 4096], P('section', 'fsdp')
- grad_qkv_weight: float32 [2, 1024, 3072], P('section', 'fsdp')
- grad_out_weight: float32 [2, 1024, 1024], P('section', 'fsdp')
- grad_fc_weight: float32 [2, 1024, 4096], P('section', 'fsdp')
- grad_proj_weight: float32 [2, 4096, 1024], P('section', 'fsdp')
The draws below stay inside these ranges and needn't reach their ends.
Inputs may be any that keep to these rules, and one draw needn't show every extreme that they name: Each sequence's positions are a permutation of 0 to 1023 made of aligned runs of 64 consecutive increasing values.
All inputs are finite; a program needn't handle non-finite values.
Results may differ from the reference program's by a relative error of at most 0.024.
Values may be sent and summed in bfloat16 or wider, within the bound.
No kernel may reach another device: no remote copies, remote signals or barrier semaphores. Data moves between devices by JAX's collectives and lax.ppermute only.
A program may use at most 384 MiB of HBM per device.

```python
import math
from functools import partial
import jax
import jax.numpy as jnp
from jax import lax

D = 1024
HD = 64
FF = 4096
MB = 2
SECTIONS = 2
SEQS = 2
LEN = 1024
PIECE = 64


def draw_positions(key, part):
    rows = MB * SEQS
    pieces = LEN // PIECE
    keys = jax.random.split(key, rows)
    order = jax.vmap(lambda one_key: jax.random.permutation(one_key, pieces))(keys).astype(jnp.int32)
    within = jnp.arange(LEN, dtype=jnp.int32)
    starts = order[:, within // PIECE]
    return (starts * PIECE + within % PIECE).reshape(MB, SEQS, LEN).astype(jnp.int32)


def steps_of(key, extent, cuts, smallest, largest):
    def one(dim, blocks):
        draws = jax.random.uniform(jax.random.fold_in(jax.random.fold_in(key, 6), dim), (blocks,), jnp.float32, smallest / len(cuts), largest / len(cuts))
        return jnp.repeat(jnp.exp(draws), extent[dim] // blocks).reshape((-1,) + (1,) * (len(extent) - dim - 1))

    level = one(*cuts[0])
    for cut in cuts[1:]:
        level = level * one(*cut)
    return level


def gaussian(rng, dims, scale, most, shards=(), held_as=jnp.bfloat16):
    loudness = steps_of(rng, dims, shards, -0.22, 0.18) if shards else 1.0
    drawn = jax.random.normal(rng, dims, jnp.float32) * scale * loudness
    return jnp.minimum(jnp.maximum(drawn, -most), most).astype(held_as)


def setup_inputs(seed: int = 0) -> dict:
    key_list = jax.random.split(jax.random.key(seed), 11)
    return {
        "inputs": gaussian(key_list[0], (MB, SEQS, LEN, D), 1.0, 6.0, ((1, 2), (2, 8))),
        "cotangent": gaussian(key_list[1], (MB, SEQS, LEN, D), 1.0, 6.0, ((1, 2), (2, 8))),
        "positions": draw_positions(jax.random.fold_in(key_list[10], 71), 0),
        "gains": jnp.clip(1.0 + 0.15 * jax.random.normal(key_list[3], (SECTIONS, 2, D), jnp.float32), 0.25, 1.75).astype(jnp.bfloat16),
        "biases": gaussian(key_list[4], (SECTIONS, 6, D), 0.5, 3.0, ((0, 2), (2, 2))),
        "fc_bias": gaussian(key_list[5], (SECTIONS, FF), 0.5, 3.0, ((0, 2), (1, 2))),
        "qkv_weight": gaussian(key_list[6], (SECTIONS, D, 3 * D), D ** -0.5, 0.1875, ((0, 2), (1, 2))),
        "out_weight": gaussian(key_list[7], (SECTIONS, D, D), (max(1, 4 * D // LEN)) ** -0.5, 3.0, ((0, 2), (1, 2))),
        "fc_weight": gaussian(key_list[8], (SECTIONS, D, FF), D ** -0.5, 0.1875, ((0, 2), (1, 2))),
        "proj_weight": gaussian(key_list[9], (SECTIONS, FF, D), FF ** -0.5, 0.09375, ((0, 2), (1, 2))),
    }


@jax.custom_vjp
def low(v):
    return lax.optimization_barrier(v.astype(jnp.bfloat16)).astype(jnp.float32)

@jax.custom_vjp
def low_back(v):
    return v

def low_keep(v):
    return (low(v), None)

def low_pass(kept, grad):
    return (grad,)

def back_keep(v):
    return (v, None)

def back_low(kept, grad):
    return (low(grad),)
low.defvjp(low_keep, low_pass)
low_back.defvjp(back_keep, back_low)
highest = lax.Precision.HIGHEST
epsilon = 1e-05

def norm_rows(values, gain, shift):
    centre = lax.optimization_barrier(jnp.mean(values, -1, keepdims=True))
    centred = values - centre
    return centred * lax.rsqrt(lax.optimization_barrier(jnp.mean(centred * centred, -1, keepdims=True)) + epsilon) * gain + shift

def attention(qkv, place):
    length = qkv.shape[0]
    model = qkv.shape[1] // 3
    heads = model // HD
    queries = qkv[:, :model].reshape(length, heads, HD)
    keys = qkv[:, model:2 * model].reshape(length, heads, HD)
    values = qkv[:, 2 * model:].reshape(length, heads, HD)
    width = math.gcd(length, 512)

    def one_block(item):
        block_q, block_pos = item
        scores = low_back(jnp.einsum('qhd,khd->hqk', block_q, keys, precision=highest) * 0.125)
        visible = place[None, None, :] <= block_pos[None, :, None]
        probs = low(jax.nn.softmax(jnp.where(visible, scores, -1e+30), axis=-1))
        return jnp.einsum('hqk,khd->qhd', probs, values, precision=highest)
    mixed = lax.map(jax.checkpoint(one_block), (queries.reshape(length // width, width, heads, HD), place.reshape(length // width, width)))
    return mixed.reshape(length, model)

def layer(params, index, values, place):
    gains, biases, fc_bias, qkv_weight, out_weight, fc_weight, proj_weight = [p[index] for p in params]
    product = partial(jnp.dot, precision=highest)
    normed = low(norm_rows(values, gains[0], biases[0]))
    shift = jnp.concatenate([biases[1], jnp.zeros_like(biases[1]), biases[2]])
    qkv = low_back(low(product(normed, qkv_weight) + shift))
    mixed = low_back(low(attention(qkv, place)))
    hidden = values + low_back(product(mixed, out_weight) + biases[3])
    second = low(norm_rows(hidden, gains[1], biases[4]))
    pre = low_back(product(second, fc_weight) + fc_bias)
    act = low(jax.nn.gelu(pre, approximate=True))
    return hidden + low_back(product(act, proj_weight) + biases[5])

def reference(inputs, cotangent, positions, gains, biases, fc_bias, qkv_weight, out_weight, fc_weight, proj_weight):
    params = tuple((p.astype(jnp.float32) for p in (gains, biases, fc_bias, qkv_weight, out_weight, fc_weight, proj_weight)))
    batch = MB * SEQS
    seqs_in = inputs.astype(jnp.float32).reshape(batch, LEN, D)
    places = positions.reshape(batch, LEN)
    extras = jnp.zeros((batch, SECTIONS - 1, LEN, D), jnp.float32)

    def forward(params, seqs_in, extras):

        def one(item):
            values, place, extra = item
            sent = []
            for index in range(SECTIONS):
                values = layer(params, index, values, place)
                if index + 1 < SECTIONS:
                    rounded = low(values)
                    sent.append(rounded)
                    values = low_back(rounded) + extra[index]
            return (values, jnp.stack(sent))
        outcome = lax.map(one, (seqs_in, places, extras))
        return (outcome[0], outcome[1])
    last, pull, sent = jax.vjp(forward, params, seqs_in, extras, has_aux=True)
    grads, grad_in, grad_extra = pull(cotangent.astype(jnp.float32).reshape(batch, LEN, D))
    rows_shape = (MB, SEQS, LEN, D)
    section_out = jnp.concatenate([jnp.moveaxis(sent, 1, 0).reshape((SECTIONS - 1,) + rows_shape), last.reshape((1,) + rows_shape)]).astype(jnp.bfloat16)
    section_grad = jnp.concatenate([grad_in.reshape((1,) + rows_shape), jnp.moveaxis(grad_extra, 1, 0).reshape((SECTIONS - 1,) + rows_shape)])
    return (section_out, section_grad, grads[0], grads[1], grads[2], grads[3], grads[4], grads[5], grads[6])
```

```python
import functools
import math

import jax
import jax.numpy as jnp
from jax import lax
from jax.experimental import pallas as pl
from jax.experimental.pallas import tpu as pltpu
from jax.sharding import PartitionSpec as P

HD = 64
EPS = 1e-05
NEG = -1e30
LOG2E = math.log2(math.e)
F32 = jnp.float32
BF16 = jnp.bfloat16
SWAP = [(0, 1), (1, 0)]


def fwd_kernel(first, last, *refs):
    if first:
        q_ref, ka_ref, kb_ref, va_ref, vb_ref, bias_ref = refs[:6]
        outs = refs[6:]
    else:
        q_ref, ka_ref, kb_ref, va_ref, vb_ref, bias_ref, st_ref, acc_ref = refs[:8]
        outs = refs[8:]
    q2 = q_ref[...] * jnp.asarray(0.125, BF16)
    k2 = jnp.concatenate([ka_ref[...], kb_ref[...]], 0)
    v2 = jnp.concatenate([va_ref[...], vb_ref[...]], 0)
    lane = lax.broadcasted_iota(jnp.int32, q2.shape, 1)
    bias = bias_ref[...]
    tops, totals, accs = [], [], []
    for h in range(2):
        qh = jnp.where((lane < HD) == (h == 0), q2, jnp.zeros_like(q2))
        s = lax.dot_general(k2, qh, (((1,), (1,)), ((), ())), preferred_element_type=F32)
        s = s * LOG2E + bias
        top = jnp.max(s, 0, keepdims=True)
        if not first:
            old = st_ref[0, h : h + 1, :]
            top = jnp.maximum(top, old)
        p = jnp.exp2(s - top)
        total = jnp.sum(p, 0, keepdims=True)
        o = lax.dot_general(
            v2, p.astype(BF16), (((0,), (0,)), ((), ())), preferred_element_type=F32
        )[h * HD : (h + 1) * HD]
        if not first:
            factor = jnp.exp2(old - top)
            total = total + factor * st_ref[0, 2 + h : 3 + h, :]
            o = o + factor * acc_ref[0, h * HD : (h + 1) * HD, :]
        tops.append(top)
        totals.append(total)
        accs.append(o)
    if last:
        o_ref, lse_ref = outs
        o = jnp.concatenate([a / t for a, t in zip(accs, totals)], 0)
        o_ref[...] = o.T.astype(BF16)
        lse_ref[0] = jnp.concatenate([t + jnp.log2(u) for t, u in zip(tops, totals)], 0)
    else:
        st_out, acc_out = outs
        st_out[0] = jnp.concatenate(tops + totals, 0)
        acc_out[0] = jnp.concatenate(accs, 0)


def attend_chunk(q, ks, vs, bias, state, last):
    rows, model = q.shape
    krows = ks[0].shape[0]
    pairs = model // (2 * HD)
    first = state is None
    col = lambda r: pl.BlockSpec((r, 2 * HD), lambda j: (0, j))
    st = lambda r: pl.BlockSpec((1, r, rows), lambda j: (j, 0, 0))
    in_specs = [col(rows), col(krows), col(krows), col(krows), col(krows)]
    in_specs.append(pl.BlockSpec(bias.shape, lambda j: (0, 0)))
    args = [q, ks[0], ks[1], vs[0], vs[1], bias]
    if not first:
        in_specs += [st(4), st(2 * HD)]
        args += list(state)
    if last:
        out_specs = [col(rows), st(2)]
        out_shape = [
            jax.ShapeDtypeStruct((rows, model), BF16),
            jax.ShapeDtypeStruct((pairs, 2, rows), F32),
        ]
    else:
        out_specs = [st(4), st(2 * HD)]
        out_shape = [
            jax.ShapeDtypeStruct((pairs, 4, rows), F32),
            jax.ShapeDtypeStruct((pairs, 2 * HD, rows), F32),
        ]
    return pl.pallas_call(
        functools.partial(fwd_kernel, first, last),
        grid=(pairs,),
        in_specs=in_specs,
        out_specs=out_specs,
        out_shape=out_shape,
        cost_estimate=pl.CostEstimate(
            flops=8 * rows * krows * model,
            bytes_accessed=12 * rows * model,
            transcendentals=2 * rows * krows * model // HD,
        ),
        name="attend",
    )(*args)


def bwd_kernel(q_ref, do_ref, o_ref, lse_ref, ka_ref, kb_ref, va_ref, vb_ref, bias_ref,
               dq_ref, dk_ref, dv_ref):
    q2 = q_ref[...] * jnp.asarray(0.125, BF16)
    do2 = do_ref[...]
    k2 = jnp.concatenate([ka_ref[...], kb_ref[...]], 0)
    v2 = jnp.concatenate([va_ref[...], vb_ref[...]], 0)
    lane = lax.broadcasted_iota(jnp.int32, q2.shape, 1)
    bias = bias_ref[...]
    prod = (o_ref[...].astype(F32) * do2.astype(F32)).T
    dk = dv = None
    dqs = []
    for h in range(2):
        mine = (lane < HD) == (h == 0)
        qh = jnp.where(mine, q2, jnp.zeros_like(q2))
        doh = jnp.where(mine, do2, jnp.zeros_like(do2))
        s = lax.dot_general(k2, qh, (((1,), (1,)), ((), ())), preferred_element_type=F32)
        p = jnp.exp2(s * LOG2E + bias - lse_ref[0, h : h + 1, :])
        dp = lax.dot_general(v2, doh, (((1,), (1,)), ((), ())), preferred_element_type=F32)
        delta = jnp.sum(prod[h * HD : (h + 1) * HD], 0, keepdims=True)
        ds = (p * (dp - delta)).astype(BF16)
        dvh = jnp.dot(p.astype(BF16), doh, preferred_element_type=F32)
        dkh = jnp.dot(ds, qh, preferred_element_type=F32)
        dv = dvh if dv is None else dv + dvh
        dk = dkh if dk is None else dk + dkh
        dqs.append(
            lax.dot_general(k2, ds, (((0,), (0,)), ((), ())), preferred_element_type=F32)[
                h * HD : (h + 1) * HD
            ]
        )
    dq_ref[...] = jnp.concatenate(dqs, 0).T * 0.125
    dk_ref[...] = dk.astype(BF16)
    dv_ref[...] = dv.astype(BF16)


def attend_chunk_back(q, do, o, lse, ks, vs, bias):
    rows, model = q.shape
    krows = ks[0].shape[0]
    pairs = model // (2 * HD)
    col = lambda r: pl.BlockSpec((r, 2 * HD), lambda j: (0, j))
    st = lambda r: pl.BlockSpec((1, r, rows), lambda j: (j, 0, 0))
    return pl.pallas_call(
        bwd_kernel,
        grid=(pairs,),
        in_specs=[col(rows), col(rows), col(rows), st(2), col(krows), col(krows), col(krows),
                  col(krows), pl.BlockSpec(bias.shape, lambda j: (0, 0))],
        out_specs=[col(rows), col(2 * krows), col(2 * krows)],
        out_shape=[
            jax.ShapeDtypeStruct((rows, model), F32),
            jax.ShapeDtypeStruct((2 * krows, model), BF16),
            jax.ShapeDtypeStruct((2 * krows, model), BF16),
        ],
        cost_estimate=pl.CostEstimate(
            flops=20 * rows * krows * model,
            bytes_accessed=20 * rows * model,
            transcendentals=2 * rows * krows * model // HD,
        ),
        name="attend_back",
    )(q, do, o, lse, ks[0], ks[1], vs[0], vs[1], bias)


def norm_parts(values):
    centre = jnp.mean(values, -1, keepdims=True)
    centred = values - centre
    recip = lax.rsqrt(jnp.mean(centred * centred, -1, keepdims=True) + EPS)
    return centred * recip, recip


def norm_back(grad, normed, recip, gain):
    inner = grad * gain
    return recip * (
        inner
        - jnp.mean(inner, -1, keepdims=True)
        - normed * jnp.mean(inner * normed, -1, keepdims=True)
    )


def half_of(a, which):
    half = a.shape[-1] // 2
    return lax.dynamic_slice_in_dim(a, which * half, half, a.ndim - 1)


def times(a, w, f):
    own, other = w
    left = jnp.dot(half_of(a, f), own, preferred_element_type=F32)
    return left + jnp.dot(half_of(a, 1 - f), other, preferred_element_type=F32)


def in_order(own, other, f, axis=-1):
    return jnp.where(
        f == 0, jnp.concatenate([own, other], axis), jnp.concatenate([other, own], axis)
    )


def times_t(a, w, f):
    contract = (((1,), (1,)), ((), ()))
    own = lax.dot_general(a, w[0], contract, preferred_element_type=F32)
    other = lax.dot_general(a, w[1], contract, preferred_element_type=F32)
    return in_order(own, other, f)


def core_swap(a):
    return lax.ppermute(a, "fsdp", SWAP)


def add(a, b):
    return (a.astype(F32) + b.astype(F32)).astype(BF16)


def line_scatter(x, z, n, pairs):
    rows = x.shape[0] // n

    def part(j):
        return lax.dynamic_slice_in_dim(x, jnp.clip(j, 0, n - 1) * rows, rows, 0)

    up = x[(n - 1) * rows :]
    down = x[:rows]
    for t in range(1, n):
        got_up = pairs(up, [(i, i + 1) for i in range(t)])
        got_down = pairs(down, [(n - 1 - i, n - 2 - i) for i in range(t)])
        up = add(got_up, part(z + n - 1 - t))
        if t < n - 1:
            down = add(got_down, part(z + t - (n - 1)))
    return add(up, got_down)


def line_gather(own, n, pairs):
    up, down = [own], [own]
    for t in range(1, n):
        up.append(pairs(up[-1], [(i, i + 1) for i in range(t - 1, n - 1)]))
        down.append(pairs(down[-1], [(i + 1, i) for i in range(0, n - t)]))
    return [own] + [up[s] + down[n - s] for s in range(1, n)]


def grid_reduce(x, c, part_y):
    n = 4
    z, y = c // 2, c % 2
    rows, cols = x.shape

    def along_z(a, links):
        perm = [(2 * i + k, 2 * j + k) for i, j in links for k in range(2)]
        return lax.ppermute(a, "ctx", perm)

    def along_y(a):
        return lax.ppermute(a, "ctx", [(i, i ^ 1) for i in range(2 * n)])

    def halves(a):
        half = a.shape[0] // 2
        keep = lax.dynamic_slice_in_dim(a, y * half, half, 0)
        send = lax.dynamic_slice_in_dim(a, (1 - y) * half, half, 0)
        return keep, send

    out = jnp.zeros((rows, cols), F32)

    def put(out, piece, at):
        return lax.dynamic_update_slice_in_dim(out, piece.astype(F32), at, 0)

    first = x[:part_y]
    keep, send = halves(first)
    mine = add(keep, along_y(send))
    second = line_scatter(x[part_y:], z, n, along_z)
    mine = line_scatter(mine, z, n, along_z)
    keep, send = halves(second)
    second = add(keep, along_y(send))
    second = in_order(second, along_y(second), y, 0)
    q2 = second.shape[0]
    q1 = mine.shape[0]
    for s, piece in enumerate(line_gather(mine, n, along_z)):
        at = jnp.mod(z - s, n) * q1
        out = put(out, piece, y * (part_y // 2) + at)
        out = put(out, along_y(piece), (1 - y) * (part_y // 2) + at)
    for s, piece in enumerate(line_gather(second, n, along_z)):
        out = put(out, piece, part_y + jnp.mod(z - s, n) * q2)
    return out


def reduce_ctx(x, c, devices):
    if devices == 8:
        return grid_reduce(x, c, x.shape[0] // 2)
    return lax.psum(x, "ctx").astype(F32)


def body(inputs, cotangent, positions, gains, biases, fc_bias, qkv_weight, out_weight, fc_weight,
         proj_weight):
    section = lax.axis_index("section")
    c = lax.axis_index("ctx")
    f = lax.axis_index("fsdp")
    devices = lax.axis_size("ctx")
    micro, _, piece, model = inputs.shape
    cores = 2
    seqs = micro * cores
    group = devices // seqs
    per = seqs // cores
    zi = c // group
    hidden_units = fc_weight.shape[2]

    def there(k):
        perm = []
        for z in range(seqs):
            for g in range(group):
                for core in range(cores):
                    to = ((z % per) ^ k) * cores + core
                    perm.append(((z * group + g) * cores + core, (to * group + g) * cores + z // per))
        return perm

    def spread(a):
        blocks = []
        for k in range(per):
            which = (zi % per) ^ k
            block = lax.dynamic_index_in_dim(a, which, 0, keepdims=False)[0]
            blocks.append(lax.ppermute(block, ("ctx", "fsdp"), there(k)))
        return jnp.concatenate(blocks, 0)

    def collect(a):
        rows = a.shape[0] // per
        blocks = []
        for k in range(per):
            perm = [(j, i) for i, j in there(k)]
            blocks.append(lax.ppermute(a[k * rows : (k + 1) * rows], ("ctx", "fsdp"), perm))
        odd = zi % per == 1
        return jnp.where(odd, jnp.stack(blocks[::-1]), jnp.stack(blocks))[:, None]

    def shift(a, r):
        perm = [
            (z * group + g, z * group + (g + r) % group) for z in range(seqs) for g in range(group)
        ]
        return lax.ppermute(a, "ctx", perm)

    places = spread(positions[..., None])[:, 0]
    x_in = spread(inputs)
    both = lambda w: (w[0], core_swap(w[0]))
    w_qkv = both(qkv_weight)
    small = jnp.concatenate([gains[0].reshape(-1), biases[0].reshape(-1), fc_bias[0]])
    small_other = core_swap(small)
    w_out = both(out_weight)
    w_fc = both(fc_weight)
    w_proj = both(proj_weight)
    top = spread(cotangent)

    half = model // 2

    def unpack(a):
        return a[: 2 * half].reshape(2, half), a[2 * half : 8 * half].reshape(6, half), a[8 * half :]

    gain_vecs, bias_vecs, fc_shift = [
        in_order(own, other, f).astype(F32) for own, other in zip(unpack(small), unpack(small_other))
    ]

    place_pair = [places, core_swap(places)]
    masks = []
    for r in range(group):
        if r == 0:
            key_place = jnp.concatenate(place_pair)
        else:
            moved = shift(places, r)
            key_place = jnp.concatenate([moved, core_swap(moved)])
        masks.append(jnp.where(key_place[:, None] <= places[None, :], 0.0, NEG).astype(F32))

    def forward(x):
        values = x.astype(F32)
        normed_a, recip_a = norm_parts(values)
        a_low = (normed_a * gain_vecs[0] + bias_vecs[0]).astype(BF16)
        qkv_shift = jnp.concatenate([bias_vecs[1], jnp.zeros_like(bias_vecs[1]), bias_vecs[2]])
        qkv = (times(a_low, w_qkv, f) + qkv_shift).astype(BF16)
        q, k, v = qkv[:, :model], qkv[:, model : 2 * model], qkv[:, 2 * model :]
        ks = [(k, core_swap(k))]
        vs = [(v, core_swap(v))]
        for r in range(1, group):
            moved = shift(k, r)
            ks.append((moved, core_swap(moved)))
            moved = shift(v, r)
            vs.append((moved, core_swap(moved)))
        state = None
        for r in range(group):
            state = attend_chunk(q, ks[r], vs[r], masks[r], state, r == group - 1)
        mixed, lse = state
        hidden = values + times(mixed, w_out, f) + bias_vecs[3]
        normed_c, recip_c = norm_parts(hidden)
        c_low = (normed_c * gain_vecs[1] + bias_vecs[4]).astype(BF16)
        pre = times(c_low, w_fc, f) + fc_shift
        act = jax.nn.gelu(pre, approximate=True).astype(BF16)
        result = hidden + times(act, w_proj, f) + bias_vecs[5]
        kept = (x, a_low, q, ks, vs, mixed, lse, hidden, c_low, pre.astype(BF16), act)
        return result.astype(BF16), kept

    def token_sum(a):
        return jnp.sum(a.astype(F32), 0)

    def backward(kept, dy_low, full):
        x, a_low, q, ks, vs, mixed, lse, hidden, c_low, pre, act = kept

        def weight_grad(left, right):
            left = jnp.concatenate([half_of(left, f), core_swap(half_of(left, 1 - f))], 0)
            right = jnp.concatenate([right, core_swap(right)], 0)
            grad = jnp.einsum("ti,to->io", left, right, preferred_element_type=F32)
            return reduce_ctx(grad.astype(BF16), c, devices)

        dy = dy_low.astype(F32)
        if full:
            grad_proj = weight_grad(act, dy_low)
        dg = times_t(dy_low, w_proj, f)
        _, gelu_back = jax.vjp(lambda u: jax.nn.gelu(u, approximate=True), pre.astype(F32))
        df = gelu_back(dg)[0].astype(BF16)
        if full:
            grad_fc = weight_grad(c_low, df)
        dc = times_t(df, w_fc, f)
        normed_c, recip_c = norm_parts(hidden)
        dh = dy + norm_back(dc, normed_c, recip_c, gain_vecs[1])
        dr = dh.astype(BF16)
        do = times_t(dr, w_out, f).astype(BF16)
        if full:
            grad_out = weight_grad(mixed, dr)
        dq = None
        rows = q.shape[0]
        dk = dv = None
        for r in list(range(1, group)) + [0]:
            part_q, part_k, part_v = attend_chunk_back(q, do, mixed, lse, ks[r], vs[r], masks[r])
            dq = part_q if dq is None else dq + part_q
            sums = []
            for part in (part_k, part_v):
                both_cores = part[:rows].astype(F32) + core_swap(part[rows:]).astype(F32)
                if r > 0:
                    both_cores = shift(both_cores.astype(BF16), group - r).astype(F32)
                sums.append(both_cores)
            dk = sums[0] if dk is None else dk + sums[0]
            dv = sums[1] if dv is None else dv + sums[1]
        dqkv = jnp.concatenate([dq, dk, dv], -1).astype(BF16)
        if full:
            grad_qkv = weight_grad(a_low, dqkv)
        da = times_t(dqkv, w_qkv, f)
        normed_a, recip_a = norm_parts(x.astype(F32))
        dx = dh + norm_back(da, normed_a, recip_a, gain_vecs[0])
        if not full:
            return dx.astype(BF16)
        sums = [
            token_sum(da * normed_a),
            token_sum(dc * normed_c),
            token_sum(da),
            token_sum(dqkv[:, :model]),
            token_sum(dqkv[:, 2 * model :]),
            token_sum(dr),
            token_sum(dc),
            token_sum(dy_low),
            token_sum(df),
        ]
        vec = jnp.concatenate(sums)
        vec = vec + core_swap(vec)
        bit = 1
        while bit < devices:
            vec = vec + lax.ppermute(vec, "ctx", [(i, i ^ bit) for i in range(devices)])
            bit *= 2
        grad_gains = half_of(vec[: 2 * model].reshape(2, model), f)
        grad_biases = half_of(vec[2 * model : 8 * model].reshape(6, model), f)
        grad_fc_bias = half_of(vec[8 * model :], f)
        return (dx.astype(BF16), grad_gains, grad_biases, grad_fc_bias, grad_qkv, grad_out, grad_fc,
                grad_proj)

    passed, _ = forward(x_in)
    arrived = lax.ppermute(passed, "section", [(0, 1)])
    result, kept = forward(jnp.where(section == 0, x_in, arrived))
    acts_out = collect(result)

    down = backward(kept, top, False)
    arrived = lax.ppermute(down, "section", [(1, 0)])
    dx, *grads = backward(kept, jnp.where(section == 0, arrived, top), True)
    grads_in = collect(dx).astype(F32)
    return (acts_out[None], grads_in[None]) + tuple(g[None] for g in grads)


def solution(mesh):
    placed = (
        P(None, "fsdp", "ctx", None),
        P(None, "fsdp", "ctx", None),
        P(None, "fsdp", "ctx"),
        P("section", None, "fsdp"),
        P("section", None, "fsdp"),
        P("section", "fsdp"),
        P("section", "fsdp", None),
        P("section", "fsdp", None),
        P("section", "fsdp", None),
        P("section", "fsdp", None),
    )
    return jax.shard_map(
        body,
        mesh=mesh,
        in_specs=placed,
        out_specs=(
            P("section", None, "fsdp", "ctx", None),
            P("section", None, "fsdp", "ctx", None),
            P("section", None, "fsdp"),
            P("section", None, "fsdp"),
            P("section", "fsdp"),
            P("section", "fsdp", None),
            P("section", "fsdp", None),
            P("section", "fsdp", None),
            P("section", "fsdp", None),
        ),
        check_vma=False,
    )
```
